32 devices in a mesh: rows: 4 (over z), vars: 8 (over y, x, core).
Axes of the slice: x: 2, y: 2, z: 4, core: 2. Of those that a mesh axis runs over, the one named last changes fastest.
Arguments:
- matrix: float32 [4096, 16384], P('rows', 'vars'), may hold values from -0.4 to 0.4
- barrier: float32 [16384], P('vars'), may hold values from 0.05 to 20
- panel_index: int32 [1], replicated, may hold values from 0 to 3
- row_offset: int32 [1], replicated, may hold values from 0 to 511
Outputs:
- factor_rows: float32 [4096, 512], P(('rows', 'vars'))
The draws below stay inside these ranges and needn't reach their ends.
All inputs are finite; a program needn't handle non-finite values.
Results may differ from the reference program's by a relative error of at most 0.000092.
Values sent between devices are 32-bit elements; how exact they have to be, the bound alone decides.
A program may use at most 64 MiB of HBM per device.

```python
import math
import jax
import jax.numpy as jnp
from jax import lax

NWIN = 16384
PANEL = 512
MROWS = 4096


def block_levels(stream_key, shape, cuts, smallest, top_value):
    level, own = 1.0, jax.random.fold_in(stream_key, 6)
    for position, parts in cuts:
        steps = jnp.exp(jax.random.uniform(jax.random.fold_in(own, position), (parts,), jnp.float32, smallest / len(cuts), top_value / len(cuts)))
        level = level * jnp.repeat(steps, shape[position] // parts).reshape([-1 if axis == position else 1 for axis in range(len(shape))])
    return level


def bell_draw(stream_key, extent, deviation, limit, cuts=(), kind=jnp.bfloat16):
    values = jax.random.normal(stream_key, extent, jnp.float32) * deviation
    if len(cuts) > 0:
        values = block_levels(stream_key, extent, cuts, -0.22, 0.18) * values
    return jnp.clip(values, min=-limit, max=limit).astype(kind)


def setup_inputs(seed: int = 0) -> dict:
    key_of = jax.random.split(jax.random.key(seed), 5)
    return {
        "matrix": bell_draw(key_of[0], (MROWS, NWIN), (6.4 / NWIN ** 0.5), 0.4, ((0, 4), (1, 8)), jnp.float32),
        "barrier": jnp.clip(jnp.exp(math.log(20.0) - 5.9914645 * jax.random.uniform(key_of[1], (NWIN,), jnp.float32) ** block_levels(key_of[1], (NWIN,), ((0, 8),), -0.2, 0.2)), 0.05, 20.0),
        "panel_index": jax.random.randint(key_of[2], (1,), 0, MROWS // (2 * PANEL)).astype(jnp.int32),
        "row_offset": jax.random.randint(key_of[3], (1,), 0, PANEL).astype(jnp.int32),
    }


def reference(matrix, barrier, panel_index, row_offset):
    first = (panel_index[0] * PANEL + row_offset[0]).astype(jnp.int32)
    picked = lax.dynamic_slice_in_dim(matrix, first, PANEL, 0)
    scaled = picked * barrier[None, :]
    normal = lax.dot_general(matrix.astype(jnp.float32), scaled.astype(jnp.float32), (((1,), (1,)), ((), ())), precision=lax.Precision.HIGHEST, preferred_element_type=jnp.float32)
    row_ids = jnp.arange(MROWS, dtype=jnp.int32)
    col_ids = jnp.arange(PANEL, dtype=jnp.int32)
    normal = normal + (row_ids[:, None] == first + col_ids[None, :]).astype(normal.dtype)
    diag_block = lax.dynamic_slice_in_dim(normal, first, PANEL, 0)
    lower = jnp.linalg.cholesky(diag_block)
    identity = jnp.eye(PANEL, dtype=normal.dtype)
    inverse = jax.scipy.linalg.solve_triangular(lower, identity, lower=True)
    result = lax.dot_general(normal.astype(jnp.float32), inverse.astype(jnp.float32), (((1,), (1,)), ((), ())), precision=lax.Precision.HIGHEST, preferred_element_type=jnp.float32)
    trailing = (row_ids >= first)[:, None]
    return jnp.where(trailing, result, jnp.zeros_like(result))
```

```python
import functools
import jax
import jax.numpy as jnp
from jax import lax
from jax.experimental import pallas as pl
from jax.experimental.pallas import tpu as pltpu
from jax.sharding import PartitionSpec as P

PANEL = 512
BLK = 128
CR = 16
F32 = jnp.float32
BF16 = jnp.bfloat16
MESH = pl.DeviceIdType.MESH
NT = (((1,), (1,)), ((), ()))


def split(x):
    hi = x.astype(BF16)
    return hi, (x - hi.astype(F32)).astype(BF16)


def shifted(ref, at, count, cols):
    base = pl.multiple_of(at // 8 * 8, 8)
    wide = ref[pl.ds(base, count + 8), cols]
    turn = lax.rem(count + 8 - (at - base), count + 8)
    return pltpu.roll(wide, turn, 0)[0:count]


def dot3(ah, al, bh, bl):
    d = functools.partial(lax.dot_general, dimension_numbers=NT, preferred_element_type=F32)
    return d(ah, bh) + (d(ah, bl) + d(al, bh))


def pick_kernel(start, a_hbm, out, wide, sem):
    rows_here = a_hbm.shape[0]
    count = BLK + 8

    def base(b):
        low = jnp.clip(start[0] + b * BLK, 0, rows_here - count)
        return pl.multiple_of(low // 8 * 8, 8)

    def copy(b):
        return pltpu.make_async_copy(a_hbm.at[pl.ds(base(b), count)], wide.at[b], sem.at[b])

    for b in range(PANEL // BLK):
        copy(b).start()
    for b in range(PANEL // BLK):
        copy(b).wait()
        at = start[0] + b * BLK
        turn = lax.rem(lax.rem(base(b) - at, count) + count, count)
        row = at + lax.broadcasted_iota(jnp.int32, (BLK, 128), 0)
        inside = (row >= 0) & (row < rows_here)
        for j in range(0, a_hbm.shape[1], 128):
            part = pltpu.roll(wide[b, :, j:j + 128], turn, 0)[0:BLK]
            out[b * BLK:(b + 1) * BLK, j:j + 128] = jnp.where(inside, part, 0.0)


def panel_kernel(
    nr, nv, nred,
    own, a_hbm, bar, n_out, d_out,
    apad, ah, al, pr, pm, ph, plo, sh, sl,
    nsend, nrecv, dsend, drecv, dsum,
    a_sem, c_send, c_recv, n_ssem, n_rsem, d_ssem, d_rsem, g_ssem, g_rsem,
):
    z = lax.axis_index("rows")
    v = lax.axis_index("vars")
    rows_here = a_hbm.shape[0]
    share = rows_here // nv
    nblk = PANEL // BLK
    cpb = BLK // CR
    dr = BLK // nred
    half = rows_here // 2

    load = pltpu.make_async_copy(a_hbm, apad, a_sem)
    load.start()

    barrier = pltpu.get_barrier_semaphore()
    for i in range(1, nv):
        pl.semaphore_signal(
            barrier, inc=1, device_id={"vars": lax.rem(v + i, nv)}, device_id_type=MESH
        )

    @pl.when(z > 0)
    def _():
        pl.semaphore_signal(barrier, inc=1, device_id={"rows": z - 1}, device_id_type=MESH)

    @pl.when(z < nr - 1)
    def _():
        pl.semaphore_signal(barrier, inc=1, device_id={"rows": z + 1}, device_id_type=MESH)

    edge = jnp.where(z > 0, 1, 0) + jnp.where(z < nr - 1, 1, 0)
    pl.semaphore_wait(barrier, nv - 1 + edge)

    load.wait()

    def chunk_copy(c):
        rows = pl.ds(pl.multiple_of(c * CR, CR), CR)
        return pltpu.make_async_remote_copy(
            src_ref=pm.at[rows], dst_ref=pr.at[rows],
            send_sem=c_send.at[c], recv_sem=c_recv.at[c],
            device_id={"rows": lax.rem(z + 1, nr)}, device_id_type=MESH,
        )

    def forward(c):
        rows = pl.ds(pl.multiple_of(c * CR, CR), CR)

        @pl.when(z > 0)
        def _():
            chunk_copy(c).wait_recv()
            pm[rows, :] = own[rows, :] + pr[rows, :]

        @pl.when(z == 0)
        def _():
            pm[rows, :] = own[rows, :]

        @pl.when(z < nr - 1)
        def _():
            chunk_copy(c).start()

        val = pm[rows, :]
        hi, lo = split(val)
        ph[rows, :] = hi
        plo[rows, :] = lo
        hi, lo = split(val * bar[...])
        sh[rows, :] = hi
        sl[rows, :] = lo

    def n_copy(b, src, dst):
        return pltpu.make_async_remote_copy(
            src_ref=nsend.at[b, dst], dst_ref=nrecv.at[b, src],
            send_sem=n_ssem.at[b, dst], recv_sem=n_rsem.at[b, src],
            device_id={"vars": dst}, device_id_type=MESH,
        )

    def d_copy(b, src, dst):
        width = BLK * (b + 1)
        return pltpu.make_async_remote_copy(
            src_ref=dsend.at[b, dst, :, pl.ds(0, width)],
            dst_ref=drecv.at[b, src, :, pl.ds(0, width)],
            send_sem=d_ssem.at[b, dst], recv_sem=d_rsem.at[b, src],
            device_id={"vars": dst}, device_id_type=MESH,
        )

    def g_copy(b, src, dst):
        width = BLK * (b + 1)
        ref = dsum.at[b, src, :, pl.ds(0, width)]
        return pltpu.make_async_remote_copy(
            src_ref=ref, dst_ref=ref,
            send_sem=g_ssem.at[b, dst], recv_sem=g_rsem.at[b, src],
            device_id={"vars": dst}, device_id_type=MESH,
        )

    def others(fn, count=None):
        @pl.loop(1, nv)
        def _(i):
            fn(lax.rem(v + i, nv))

    def diag_part(b):
        rows = pl.ds(b * BLK, BLK)
        for j in range(b + 1):
            cols = pl.ds(j * BLK, BLK)
            d = dot3(sh[rows, :], sl[rows, :], ph[cols, :], plo[cols, :])
            dsend[b, :, :, cols] = d.reshape(nred, dr, BLK)

        def send(dst):
            @pl.when(dst < nred)
            def _():
                d_copy(b, v, dst).start()

        others(send)

    def diag_reduce(b):
        width = BLK * (b + 1)

        @pl.when(v < nred)
        def _():
            dsum[b, v, :, pl.ds(0, width)] = dsend[b, v, :, pl.ds(0, width)]

            def add(src):
                d_copy(b, src, v).wait_recv()
                dsum[b, v, :, pl.ds(0, width)] += drecv[b, src, :, pl.ds(0, width)]

            others(add)
            others(lambda dst: g_copy(b, v, dst).start())

    def diag_finish(b):
        width = BLK * (b + 1)

        def get(src):
            @pl.when(src < nred)
            def _():
                g_copy(b, src, v).wait_recv()

        others(get)
        if width < PANEL:
            d_out[pl.ds(b * BLK, BLK), pl.ds(width, PANEL - width)] = jnp.zeros(
                (BLK, PANEL - width), F32
            )
        d_out[pl.ds(b * BLK, BLK), pl.ds(0, width)] = dsum[b, :, :, pl.ds(0, width)].reshape(
            BLK, width
        )

    def product(b, part):
        rows = pl.ds(b * BLK, BLK)
        arows = pl.ds(part * half, half)
        n = dot3(ah[arows, :], al[arows, :], sh[rows, :], sl[rows, :])
        per = nv // 2
        nsend[b, pl.ds(part * per, per)] = n.reshape(per, share, BLK)

        @pl.loop(part * per, (part + 1) * per)
        def _(dst):
            @pl.when(dst != v)
            def _():
                n_copy(b, v, dst).start()

    def n_finish(b):
        cols = pl.ds(b * BLK, BLK)
        n_out[:, cols] = nsend[b, v]

        def add(src):
            n_copy(b, src, v).wait_recv()
            n_out[:, cols] += nrecv[b, src]

        others(add)

    per_step = rows_here // cpb
    for b in range(nblk + 1):
        if b < nblk:
            @pl.loop(0, cpb // 2)
            def _(i):
                forward(b * cpb + i)
                if b == 0:
                    for k in range(2):
                        at = (i * 2 + k) * per_step
                        hi, lo = split(apad[pl.ds(pl.multiple_of(at, per_step), per_step), :])
                        rows = pl.ds(pl.multiple_of(at, per_step), per_step)
                        ah[rows, :] = hi
                        al[rows, :] = lo
        if b > 0:
            diag_part(b - 1)
            product(b - 1, 0)
        if b < nblk:
            @pl.loop(cpb // 2, cpb)
            def _(i):
                forward(b * cpb + i)
        if b > 0:
            diag_reduce(b - 1)
            product(b - 1, 1)
        if b > 1:
            diag_finish(b - 2)
            n_finish(b - 2)
    diag_finish(nblk - 1)
    n_finish(nblk - 1)

    @pl.when(z < nr - 1)
    def _():
        @pl.loop(0, PANEL // CR)
        def _(c):
            chunk_copy(c).wait_send()

    for b in range(nblk):
        def drain(dst):
            n_copy(b, v, dst).wait_send()

            @pl.when(dst < nred)
            def _():
                d_copy(b, v, dst).wait_send()

            @pl.when(v < nred)
            def _():
                g_copy(b, v, dst).wait_send()

        others(drain)


def dot6(a, b, dims):
    return lax.dot_general(
        a, b, (dims, ((), ())), precision=lax.Precision.HIGHEST, preferred_element_type=F32
    )


def factor_kernel(share, pos, n_ref, d_ref, o_ref, lpad, ws, wm, inv):
    first_to_own = pos[0]
    nblk = PANEL // BLK
    row_id = lax.broadcasted_iota(jnp.int32, (BLK, BLK), 0)
    col_id = lax.broadcasted_iota(jnp.int32, (BLK, BLK), 1)
    eye = (row_id == col_id).astype(F32)
    lpad[...] = jnp.zeros_like(lpad)
    own_id = lax.broadcasted_iota(jnp.int32, (share, BLK), 0) + first_to_own
    below = own_id >= PANEL
    xs = []
    for b in range(nblk):
        rows = pl.ds(share + b * BLK, BLK)
        cols = slice(b * BLK, (b + 1) * BLK)
        for j in range(b):
            acc = d_ref[b * BLK:(b + 1) * BLK, j * BLK:(j + 1) * BLK]
            for i in range(j):
                acc -= dot6(
                    lpad[rows, i * BLK:(i + 1) * BLK],
                    lpad[pl.ds(share + j * BLK, BLK), i * BLK:(i + 1) * BLK],
                    ((1,), (1,)),
                )
            lpad[rows, j * BLK:(j + 1) * BLK] = dot6(acc, inv[j], ((1,), (1,)))
        acc = d_ref[b * BLK:(b + 1) * BLK, cols] + eye
        if b > 0:
            left = lpad[rows, 0:b * BLK]
            acc -= dot6(left, left, ((1,), (1,)))

        def column(k, carry):
            s, m, scale = carry
            col = jnp.sum(jnp.where(col_id == k, s, 0.0), axis=1, keepdims=True)
            ws[...] = s
            wm[...] = m
            srow = ws[pl.ds(k, 1), :]
            mrow = wm[pl.ds(k, 1), :]
            pivot = jnp.sum(jnp.where(col_id[0:1, :] == k, srow, 0.0), axis=1, keepdims=True)
            root = lax.rsqrt(pivot)
            root = root * (1.5 - 0.5 * pivot * root * root)
            low = row_id[:, 0:1] > k
            factor = jnp.where(low, col * (root * root), 0.0)
            scale = jnp.where(row_id[:, 0:1] == k, root, scale)
            return s - factor * srow, m - factor * mrow, scale

        s, m, scale = lax.fori_loop(0, BLK, column, (acc, eye, jnp.ones((BLK, 1), F32)))
        upper = jnp.where(row_id <= col_id, s, 0.0) * scale
        inv[b] = m * scale
        lpad[rows, cols] = upper.T
        x = n_ref[:, cols]
        for i in range(b):
            x -= dot6(xs[i], lpad[rows, i * BLK:(i + 1) * BLK], ((1,), (1,)))
        xs.append(dot6(x, inv[b], ((1,), (1,))))
    at = share + jnp.clip(first_to_own, -share, PANEL)
    for b in range(nblk):
        cols = slice(b * BLK, (b + 1) * BLK)
        o_ref[:, cols] = jnp.where(below, xs[b], 0.0) + shifted(lpad, at, share, cols)


def body(nr, nv, matrix, barrier, panel_index, row_offset):
    rows_here, vloc = matrix.shape
    share = rows_here // nv
    nblk = PANEL // BLK
    nred = min(nv, BLK // 8)
    dr = BLK // nred
    first = panel_index * PANEL + row_offset
    vm = pl.BlockSpec(memory_space=pltpu.VMEM)
    sm = pl.BlockSpec(memory_space=pltpu.SMEM)
    dma = pltpu.SemaphoreType.DMA
    nchunk = PANEL // CR
    picked = pl.pallas_call(
        pick_kernel,
        out_shape=jax.ShapeDtypeStruct((PANEL, vloc), F32),
        in_specs=[sm, pl.BlockSpec(memory_space=pl.ANY)],
        out_specs=vm,
        scratch_shapes=[
            pltpu.VMEM((nblk, BLK + 8, vloc), F32),
            dma((nblk,)),
        ],
        compiler_params=pltpu.CompilerParams(vmem_limit_bytes=32 << 20),
        name="pick",
    )(first - lax.axis_index("rows") * rows_here, matrix)
    n, d = pl.pallas_call(
        functools.partial(panel_kernel, nr, nv, nred),
        out_shape=(
            jax.ShapeDtypeStruct((share, PANEL), F32),
            jax.ShapeDtypeStruct((PANEL, PANEL), F32),
        ),
        in_specs=[vm, pl.BlockSpec(memory_space=pl.ANY), vm],
        out_specs=(vm, vm),
        scratch_shapes=[
            pltpu.VMEM((rows_here, vloc), F32),
            pltpu.VMEM((rows_here, vloc), BF16),
            pltpu.VMEM((rows_here, vloc), BF16),
            pltpu.VMEM((PANEL, vloc), F32),
            pltpu.VMEM((PANEL, vloc), F32),
            pltpu.VMEM((PANEL, vloc), BF16),
            pltpu.VMEM((PANEL, vloc), BF16),
            pltpu.VMEM((PANEL, vloc), BF16),
            pltpu.VMEM((PANEL, vloc), BF16),
            pltpu.VMEM((nblk, nv, share, BLK), F32),
            pltpu.VMEM((nblk, nv, share, BLK), F32),
            pltpu.VMEM((nblk, nred, dr, PANEL), F32),
            pltpu.VMEM((nblk, nv, dr, PANEL), F32),
            pltpu.VMEM((nblk, nred, dr, PANEL), F32),
            dma,
            dma((nchunk,)),
            dma((nchunk,)),
            dma((nblk, nv)),
            dma((nblk, nv)),
            dma((nblk, nv)),
            dma((nblk, nv)),
            dma((nblk, nv)),
            dma((nblk, nv)),
        ],
        compiler_params=pltpu.CompilerParams(
            collective_id=0, has_side_effects=True, vmem_limit_bytes=60 << 20
        ),
        name="panel_sums",
    )(picked, matrix, barrier.reshape(1, vloc))
    own = lax.axis_index("rows") * rows_here + lax.axis_index("vars") * share
    return pl.pallas_call(
        functools.partial(factor_kernel, share),
        out_shape=jax.ShapeDtypeStruct((share, PANEL), F32),
        in_specs=[sm, vm, vm],
        out_specs=vm,
        scratch_shapes=[
            pltpu.VMEM((PANEL + 2 * share + 8, PANEL), F32),
            pltpu.VMEM((BLK, BLK), F32),
            pltpu.VMEM((BLK, BLK), F32),
            pltpu.VMEM((nblk, BLK, BLK), F32),
        ],
        compiler_params=pltpu.CompilerParams(vmem_limit_bytes=32 << 20),
        name="factor",
    )(own - first, n, d)


def solution(mesh):
    return jax.shard_map(
        functools.partial(body, mesh.shape["rows"], mesh.shape["vars"]),
        mesh=mesh,
        in_specs=(P("rows", "vars"), P("vars"), P(), P()),
        out_specs=P(("rows", "vars"), None),
        check_vma=False,
    )
```

```python
import functools
import jax
import jax.numpy as jnp
from jax import lax
from jax.experimental import pallas as pl
from jax.experimental.pallas import tpu as pltpu
from jax.sharding import PartitionSpec as P

PANEL = 512
BLK = 128
CR = 16
GRP = 16
F32 = jnp.float32
BF16 = jnp.bfloat16
MESH = pl.DeviceIdType.MESH
NT = (((1,), (1,)), ((), ()))


def split(x):
    hi = x.astype(BF16)
    return hi, (x - hi.astype(F32)).astype(BF16)


def shifted(ref, at, count, cols):
    base = pl.multiple_of(at // 8 * 8, 8)
    wide = ref[pl.ds(base, count + 8), cols]
    turn = lax.rem(count + 8 - (at - base), count + 8)
    return pltpu.roll(wide, turn, 0)[0:count]


def dot3(ah, al, bh, bl):
    d = functools.partial(lax.dot_general, dimension_numbers=NT, preferred_element_type=F32)
    return d(ah, bh) + (d(ah, bl) + d(al, bh))


def dot6(a, b, dims):
    return lax.dot_general(
        a, b, (dims, ((), ())), precision=lax.Precision.HIGHEST, preferred_element_type=F32
    )


def eliminate(k, ws, wm):
    rows = pl.ds(pl.multiple_of(k, GRP), GRP)
    s = ws[rows, :]
    m = wm[rows, :]
    turned = pltpu.roll(s, lax.rem(BLK - k, BLK), 1)
    cols = [jnp.broadcast_to(turned[:, t:t + 1], (GRP, BLK)) for t in range(GRP)]
    row_id = lax.broadcasted_iota(jnp.int32, (GRP, BLK), 0)
    lane_id = lax.broadcasted_iota(jnp.int32, (GRP, BLK), 1)
    root = jnp.ones((GRP, BLK), F32)
    for t in range(GRP):
        pivot = cols[t][t:t + 1, :]
        r = lax.rsqrt(pivot)
        r = r * (1.5 - 0.5 * pivot * r * r)
        rr = r * r
        factor = jnp.where(row_id > t, cols[t] * rr, 0.0)
        root = jnp.where(row_id == t, r, root)
        for u in range(t + 1, GRP):
            cols[u] = cols[u] - factor * cols[u][t:t + 1, :]
        s = s - factor * s[t:t + 1, :]
        m = m - factor * m[t:t + 1, :]
    s = jnp.where(lane_id >= k, s * root, 0.0)
    m = m * root
    ws[...] -= dot6(s, s, ((0,), (0,)))
    wm[...] -= dot6(s, m, ((0,), (0,)))
    ws[rows, :] = s
    wm[rows, :] = m


def factor_start(b, diag, lower, inv, ws, wm):
    rows = pl.ds(b * BLK, BLK)
    row_id = lax.broadcasted_iota(jnp.int32, (BLK, BLK), 0)
    col_id = lax.broadcasted_iota(jnp.int32, (BLK, BLK), 1)
    eye = (row_id == col_id).astype(F32)
    for j in range(b):
        cols = pl.ds(j * BLK, BLK)
        acc = diag(j)
        if j > 0:
            left = pl.ds(0, j * BLK)
            acc -= dot6(lower[rows, left], lower[cols, left], ((1,), (1,)))
        lower[rows, cols] = dot6(acc, inv[j], ((1,), (1,)))
    acc = diag(b) + eye
    if b > 0:
        left = lower[rows, 0:b * BLK]
        acc -= dot6(left, left, ((1,), (1,)))
    ws[...] = acc
    wm[...] = eye


def factor_end(b, lower, inv, ws, wm):
    rows = pl.ds(b * BLK, BLK)
    row_id = lax.broadcasted_iota(jnp.int32, (BLK, BLK), 0)
    col_id = lax.broadcasted_iota(jnp.int32, (BLK, BLK), 1)
    inv[b] = wm[...]
    lower[rows, pl.ds(b * BLK, BLK)] = jnp.where(row_id <= col_id, ws[...], 0.0).T
    rest = PANEL - (b + 1) * BLK
    if rest > 0:
        lower[rows, pl.ds((b + 1) * BLK, rest)] = jnp.zeros((BLK, rest), F32)


def pick_kernel(start, a_hbm, out, wide, sem):
    rows_here = a_hbm.shape[0]
    count = BLK + 8

    def base(b):
        low = jnp.clip(start[0] + b * BLK, 0, rows_here - count)
        return pl.multiple_of(low // 8 * 8, 8)

    def copy(b):
        return pltpu.make_async_copy(a_hbm.at[pl.ds(base(b), count)], wide.at[b], sem.at[b])

    for b in range(PANEL // BLK):
        copy(b).start()
    for b in range(PANEL // BLK):
        copy(b).wait()
        at = start[0] + b * BLK
        turn = lax.rem(lax.rem(base(b) - at, count) + count, count)
        row = at + lax.broadcasted_iota(jnp.int32, (BLK, 128), 0)
        inside = (row >= 0) & (row < rows_here)
        for j in range(0, a_hbm.shape[1], 128):
            part = pltpu.roll(wide[b, :, j:j + 128], turn, 0)[0:BLK]
            out[b * BLK:(b + 1) * BLK, j:j + 128] = jnp.where(inside, part, 0.0)


def panel_kernel(
    nr, nv, nred,
    own, a_hbm, bar, x_out, lower,
    apad, ah, al, pr, pm, ph, plo, sh, sl,
    nsend, nrecv, dsend, drecv, dsum, ws, wm, inv,
    a_sem, c_send, c_recv, n_ssem, n_rsem, d_ssem, d_rsem, g_ssem, g_rsem,
):
    z = lax.axis_index("rows")
    v = lax.axis_index("vars")
    rows_here = a_hbm.shape[0]
    share = rows_here // nv
    nblk = PANEL // BLK
    cpb = BLK // CR
    dr = BLK // nred
    half = rows_here // 2

    load = pltpu.make_async_copy(a_hbm, apad, a_sem)
    load.start()

    barrier = pltpu.get_barrier_semaphore()
    for i in range(1, nv):
        pl.semaphore_signal(
            barrier, inc=1, device_id={"vars": lax.rem(v + i, nv)}, device_id_type=MESH
        )

    @pl.when(z > 0)
    def _():
        pl.semaphore_signal(barrier, inc=1, device_id={"rows": z - 1}, device_id_type=MESH)

    @pl.when(z < nr - 1)
    def _():
        pl.semaphore_signal(barrier, inc=1, device_id={"rows": z + 1}, device_id_type=MESH)

    edge = jnp.where(z > 0, 1, 0) + jnp.where(z < nr - 1, 1, 0)
    pl.semaphore_wait(barrier, nv - 1 + edge)

    load.wait()

    def chunk_copy(c):
        rows = pl.ds(pl.multiple_of(c * CR, CR), CR)
        return pltpu.make_async_remote_copy(
            src_ref=pm.at[rows], dst_ref=pr.at[rows],
            send_sem=c_send.at[c], recv_sem=c_recv.at[c],
            device_id={"rows": lax.rem(z + 1, nr)}, device_id_type=MESH,
        )

    def forward(c):
        rows = pl.ds(pl.multiple_of(c * CR, CR), CR)

        @pl.when(z > 0)
        def _():
            chunk_copy(c).wait_recv()
            pm[rows, :] = own[rows, :] + pr[rows, :]

        @pl.when(z == 0)
        def _():
            pm[rows, :] = own[rows, :]

        @pl.when(z < nr - 1)
        def _():
            chunk_copy(c).start()

        val = pm[rows, :]
        hi, lo = split(val)
        ph[rows, :] = hi
        plo[rows, :] = lo
        hi, lo = split(val * bar[...])
        sh[rows, :] = hi
        sl[rows, :] = lo

    def n_copy(b, src, dst):
        return pltpu.make_async_remote_copy(
            src_ref=nsend.at[b, dst], dst_ref=nrecv.at[b, src],
            send_sem=n_ssem.at[b, dst], recv_sem=n_rsem.at[b, src],
            device_id={"vars": dst}, device_id_type=MESH,
        )

    def d_copy(b, src, dst):
        width = BLK * (b + 1)
        return pltpu.make_async_remote_copy(
            src_ref=dsend.at[b, dst, :, pl.ds(0, width)],
            dst_ref=drecv.at[b, src, :, pl.ds(0, width)],
            send_sem=d_ssem.at[b, dst], recv_sem=d_rsem.at[b, src],
            device_id={"vars": dst}, device_id_type=MESH,
        )

    def g_copy(b, src, dst):
        width = BLK * (b + 1)
        ref = dsum.at[b, src, :, pl.ds(0, width)]
        return pltpu.make_async_remote_copy(
            src_ref=ref, dst_ref=ref,
            send_sem=g_ssem.at[b, dst], recv_sem=g_rsem.at[b, src],
            device_id={"vars": dst}, device_id_type=MESH,
        )

    def others(fn, count=None):
        @pl.loop(1, nv)
        def _(i):
            fn(lax.rem(v + i, nv))

    def diag_part(b):
        rows = pl.ds(b * BLK, BLK)
        for j in range(b + 1):
            cols = pl.ds(j * BLK, BLK)
            d = dot3(sh[rows, :], sl[rows, :], ph[cols, :], plo[cols, :])
            dsend[b, :, :, cols] = d.reshape(nred, dr, BLK)

        def send(dst):
            @pl.when(dst < nred)
            def _():
                d_copy(b, v, dst).start()

        others(send)

    def diag_reduce(b):
        width = BLK * (b + 1)

        @pl.when(v < nred)
        def _():
            dsum[b, v, :, pl.ds(0, width)] = dsend[b, v, :, pl.ds(0, width)]

            def add(src):
                d_copy(b, src, v).wait_recv()
                dsum[b, v, :, pl.ds(0, width)] += drecv[b, src, :, pl.ds(0, width)]

            others(add)
            others(lambda dst: g_copy(b, v, dst).start())

    def diag_finish(b):
        def get(src):
            @pl.when(src < nred)
            def _():
                g_copy(b, src, v).wait_recv()

        others(get)

        def diag(j):
            return dsum[b, :, :, pl.ds(j * BLK, BLK)].reshape(BLK, BLK)

        factor_start(b, diag, lower, inv, ws, wm)

    def product(b, part):
        rows = pl.ds(b * BLK, BLK)
        arows = pl.ds(part * half, half)
        n = dot3(ah[arows, :], al[arows, :], sh[rows, :], sl[rows, :])
        per = nv // 2
        nsend[b, pl.ds(part * per, per)] = n.reshape(per, share, BLK)

        @pl.loop(part * per, (part + 1) * per)
        def _(dst):
            @pl.when(dst != v)
            def _():
                n_copy(b, v, dst).start()

    def solve(b):
        def add(src):
            n_copy(b, src, v).wait_recv()
            nsend[b, v] += nrecv[b, src]

        others(add)
        x = nsend[b, v]
        if b > 0:
            left = pl.ds(0, b * BLK)
            x -= dot6(x_out[:, left], lower[pl.ds(b * BLK, BLK), left], ((1,), (1,)))
        x_out[:, pl.ds(b * BLK, BLK)] = dot6(x, inv[b], ((1,), (1,)))

    def steps(b, low, high, also=None):
        @pl.loop(low, high)
        def _(i):
            if b < nblk:
                forward(b * cpb + i)
            if also is not None:
                also(i)

    def halves(i):
        for k in range(2):
            at = pl.multiple_of((i * 2 + k) * per_step, per_step)
            rows = pl.ds(at, per_step)
            hi, lo = split(apad[rows, :])
            ah[rows, :] = hi
            al[rows, :] = lo

    per_step = rows_here // cpb
    mid = cpb // 2
    groups = BLK // GRP // (cpb - mid)
    steps(0, 0, mid, halves)
    steps(0, mid, cpb)
    for b in range(1, nblk + 1):
        diag_part(b - 1)
        steps(b, 0, 2)
        product(b - 1, 0)
        steps(b, 2, 3)
        diag_reduce(b - 1)
        steps(b, 3, mid)
        product(b - 1, 1)
        diag_finish(b - 1)

        def columns(i):
            for g in range(groups):
                eliminate(((i - mid) * groups + g) * GRP, ws, wm)

        steps(b, mid, cpb, columns)
        factor_end(b - 1, lower, inv, ws, wm)
        solve(b - 1)

    @pl.when(z < nr - 1)
    def _():
        @pl.loop(0, PANEL // CR)
        def _(c):
            chunk_copy(c).wait_send()

    for b in range(nblk):
        def drain(dst):
            n_copy(b, v, dst).wait_send()

            @pl.when(dst < nred)
            def _():
                d_copy(b, v, dst).wait_send()

            @pl.when(v < nred)
            def _():
                g_copy(b, v, dst).wait_send()

        others(drain)


def finish_kernel(share, pos, x_ref, l_hbm, o_ref, wide, sem):
    count = share + 8
    low = jnp.clip(pos[0], 0, PANEL - count)
    base = pl.multiple_of(low // 8 * 8, 8)
    copy = pltpu.make_async_copy(l_hbm.at[pl.ds(base, count)], wide, sem)
    copy.start()
    copy.wait()
    turn = lax.rem(lax.rem(base - pos[0], count) + count, count)
    row = pos[0] + lax.broadcasted_iota(jnp.int32, (share, 128), 0)
    inside = (row >= 0) & (row < PANEL)
    for j in range(0, PANEL, 128):
        part = pltpu.roll(wide[:, j:j + 128], turn, 0)[0:share]
        x = jnp.where(row >= PANEL, x_ref[:, j:j + 128], 0.0)
        o_ref[:, j:j + 128] = jnp.where(inside, part, x)


def body(nr, nv, matrix, barrier, panel_index, row_offset):
    rows_here, vloc = matrix.shape
    share = rows_here // nv
    nblk = PANEL // BLK
    nred = min(nv, BLK // 8)
    dr = BLK // nred
    first = panel_index * PANEL + row_offset
    vm = pl.BlockSpec(memory_space=pltpu.VMEM)
    sm = pl.BlockSpec(memory_space=pltpu.SMEM)
    dma = pltpu.SemaphoreType.DMA
    nchunk = PANEL // CR
    picked = pl.pallas_call(
        pick_kernel,
        out_shape=jax.ShapeDtypeStruct((PANEL, vloc), F32),
        in_specs=[sm, pl.BlockSpec(memory_space=pl.ANY)],
        out_specs=vm,
        scratch_shapes=[
            pltpu.VMEM((nblk, BLK + 8, vloc), F32),
            dma((nblk,)),
        ],
        compiler_params=pltpu.CompilerParams(vmem_limit_bytes=32 << 20),
        name="pick",
    )(first - lax.axis_index("rows") * rows_here, matrix)
    x, low = pl.pallas_call(
        functools.partial(panel_kernel, nr, nv, nred),
        out_shape=(
            jax.ShapeDtypeStruct((share, PANEL), F32),
            jax.ShapeDtypeStruct((PANEL, PANEL), F32),
        ),
        in_specs=[vm, pl.BlockSpec(memory_space=pl.ANY), vm],
        out_specs=(vm, vm),
        scratch_shapes=[
            pltpu.VMEM((rows_here, vloc), F32),
            pltpu.VMEM((rows_here, vloc), BF16),
            pltpu.VMEM((rows_here, vloc), BF16),
            pltpu.VMEM((PANEL, vloc), F32),
            pltpu.VMEM((PANEL, vloc), F32),
            pltpu.VMEM((PANEL, vloc), BF16),
            pltpu.VMEM((PANEL, vloc), BF16),
            pltpu.VMEM((PANEL, vloc), BF16),
            pltpu.VMEM((PANEL, vloc), BF16),
            pltpu.VMEM((nblk, nv, share, BLK), F32),
            pltpu.VMEM((nblk, nv, share, BLK), F32),
            pltpu.VMEM((nblk, nred, dr, PANEL), F32),
            pltpu.VMEM((nblk, nv, dr, PANEL), F32),
            pltpu.VMEM((nblk, nred, dr, PANEL), F32),
            pltpu.VMEM((BLK, BLK), F32),
            pltpu.VMEM((BLK, BLK), F32),
            pltpu.VMEM((nblk, BLK, BLK), F32),
            dma,
            dma((nchunk,)),
            dma((nchunk,)),
            dma((nblk, nv)),
            dma((nblk, nv)),
            dma((nblk, nv)),
            dma((nblk, nv)),
            dma((nblk, nv)),
            dma((nblk, nv)),
        ],
        compiler_params=pltpu.CompilerParams(
            collective_id=0, has_side_effects=True, vmem_limit_bytes=60 << 20
        ),
        name="panel_sums",
    )(picked, matrix, barrier.reshape(1, vloc))
    own = lax.axis_index("rows") * rows_here + lax.axis_index("vars") * share
    return pl.pallas_call(
        functools.partial(finish_kernel, share),
        out_shape=jax.ShapeDtypeStruct((share, PANEL), F32),
        in_specs=[sm, vm, pl.BlockSpec(memory_space=pl.ANY)],
        out_specs=vm,
        scratch_shapes=[pltpu.VMEM((share + 8, PANEL), F32), dma],
        name="finish",
    )(own - first, x, low)


def solution(mesh):
    return jax.shard_map(
        functools.partial(body, mesh.shape["rows"], mesh.shape["vars"]),
        mesh=mesh,
        in_specs=(P("rows", "vars"), P("vars"), P(), P()),
        out_specs=P(("rows", "vars"), None),
        check_vma=False,
    )
```

```python
import functools
import jax
import jax.numpy as jnp
from jax import lax
from jax.experimental import pallas as pl
from jax.experimental.pallas import tpu as pltpu
from jax.sharding import PartitionSpec as P

PANEL = 512
BLK = 128
CR = 16
GRP = 16
F32 = jnp.float32
BF16 = jnp.bfloat16
MESH = pl.DeviceIdType.MESH
NT = (((1,), (1,)), ((), ()))


def split(x):
    hi = x.astype(BF16)
    return hi, (x - hi.astype(F32)).astype(BF16)


def dot(a, b):
    return lax.dot_general(a, b, NT, preferred_element_type=F32)


def dot6(a, b, dims):
    return lax.dot_general(
        a, b, (dims, ((), ())), precision=lax.Precision.HIGHEST, preferred_element_type=F32
    )


def eliminate(k, ws, wm):
    rows = pl.ds(pl.multiple_of(k, GRP), GRP)
    s = ws[rows, :]
    m = wm[rows, :]
    turned = pltpu.roll(s, lax.rem(BLK - k, BLK), 1)
    cols = [jnp.broadcast_to(turned[:, t:t + 1], (GRP, BLK)) for t in range(GRP)]
    row_id = lax.broadcasted_iota(jnp.int32, (GRP, BLK), 0)
    lane_id = lax.broadcasted_iota(jnp.int32, (GRP, BLK), 1)
    root = jnp.ones((GRP, BLK), F32)
    for t in range(GRP):
        pivot = cols[t][t:t + 1, :]
        r = lax.rsqrt(pivot)
        r = r * (1.5 - 0.5 * pivot * r * r)
        rr = r * r
        factor = jnp.where(row_id > t, cols[t] * rr, 0.0)
        root = jnp.where(row_id == t, r, root)
        for u in range(t + 1, GRP):
            cols[u] = cols[u] - factor * cols[u][t:t + 1, :]
        s = s - factor * s[t:t + 1, :]
        m = m - factor * m[t:t + 1, :]
    s = jnp.where(lane_id >= k, s * root, 0.0)
    m = m * root
    ws[...] -= dot6(s, s, ((0,), (0,)))
    wm[...] -= dot6(s, m, ((0,), (0,)))
    ws[rows, :] = s
    wm[rows, :] = m


def factor_start(b, diag, lower, inv, ws, wm):
    rows = pl.ds(b * BLK, BLK)
    row_id = lax.broadcasted_iota(jnp.int32, (BLK, BLK), 0)
    col_id = lax.broadcasted_iota(jnp.int32, (BLK, BLK), 1)
    eye = (row_id == col_id).astype(F32)
    for j in range(b):
        cols = pl.ds(j * BLK, BLK)
        acc = diag(j)
        if j > 0:
            left = pl.ds(0, j * BLK)
            acc -= dot6(lower[rows, left], lower[cols, left], ((1,), (1,)))
        lower[rows, cols] = dot6(acc, inv[j], ((1,), (1,)))
    acc = diag(b) + eye
    if b > 0:
        left = lower[rows, 0:b * BLK]
        acc -= dot6(left, left, ((1,), (1,)))
    ws[...] = acc
    wm[...] = eye


def factor_end(b, lower, inv, ws, wm):
    rows = pl.ds(b * BLK, BLK)
    row_id = lax.broadcasted_iota(jnp.int32, (BLK, BLK), 0)
    col_id = lax.broadcasted_iota(jnp.int32, (BLK, BLK), 1)
    inv[b] = wm[...]
    lower[rows, pl.ds(b * BLK, BLK)] = jnp.where(row_id <= col_id, ws[...], 0.0).T
    rest = PANEL - (b + 1) * BLK
    if rest > 0:
        lower[rows, pl.ds((b + 1) * BLK, rest)] = jnp.zeros((BLK, rest), F32)


def pick_kernel(start, a_hbm, out, wide, sem):
    rows_here = a_hbm.shape[0]
    count = BLK + 8

    def base(b):
        low = jnp.clip(start[0] + b * BLK, 0, rows_here - count)
        return pl.multiple_of(low // 8 * 8, 8)

    def copy(b):
        return pltpu.make_async_copy(a_hbm.at[pl.ds(base(b), count)], wide.at[b], sem.at[b])

    for b in range(PANEL // BLK):
        copy(b).start()
    for b in range(PANEL // BLK):
        copy(b).wait()
        at = start[0] + b * BLK
        turn = lax.rem(lax.rem(base(b) - at, count) + count, count)
        row = at + lax.broadcasted_iota(jnp.int32, (BLK, 128), 0)
        inside = (row >= 0) & (row < rows_here)
        for j in range(0, a_hbm.shape[1], 128):
            part = pltpu.roll(wide[b, :, j:j + 128], turn, 0)[0:BLK]
            out[b * BLK:(b + 1) * BLK, j:j + 128] = jnp.where(inside, part, 0.0)


def panel_kernel(
    nr, nv, nred,
    own, a_hbm, bar, x_out, lower,
    apad, ah, al, pr, pm, ph, plo, sc,
    nsend, nrecv, dsend, drecv, dsum, ws, wm, inv,
    a_sem, o_sem, c_send, c_recv, n_ssem, n_rsem, d_ssem, d_rsem, g_ssem, g_rsem,
):
    z = lax.axis_index("rows")
    v = lax.axis_index("vars")
    rows_here = a_hbm.shape[0]
    share = rows_here // nv
    nblk = PANEL // BLK
    cpb = BLK // CR
    dr = BLK // nred
    half = rows_here // 2

    load = pltpu.make_async_copy(a_hbm, apad, a_sem)
    load.start()

    def own_copy(b):
        rows = pl.ds(b * BLK, BLK)
        return pltpu.make_async_copy(own.at[rows], pm.at[rows], o_sem.at[b])

    for b in range(nblk):
        own_copy(b).start()

    barrier = pltpu.get_barrier_semaphore()
    for i in range(1, nv):
        pl.semaphore_signal(
            barrier, inc=1, device_id={"vars": lax.rem(v + i, nv)}, device_id_type=MESH
        )

    @pl.when(z > 0)
    def _():
        pl.semaphore_signal(barrier, inc=1, device_id={"rows": z - 1}, device_id_type=MESH)

    @pl.when(z < nr - 1)
    def _():
        pl.semaphore_signal(barrier, inc=1, device_id={"rows": z + 1}, device_id_type=MESH)

    edge = jnp.where(z > 0, 1, 0) + jnp.where(z < nr - 1, 1, 0)
    pl.semaphore_wait(barrier, nv - 1 + edge)


    def chunk_copy(c):
        rows = pl.ds(pl.multiple_of(c * CR, CR), CR)
        return pltpu.make_async_remote_copy(
            src_ref=pm.at[rows], dst_ref=pr.at[rows],
            send_sem=c_send.at[c], recv_sem=c_recv.at[c],
            device_id={"rows": lax.rem(z + 1, nr)}, device_id_type=MESH,
        )

    def forward(b, i):
        c = b * cpb + i
        rows = pl.ds(pl.multiple_of(c * CR, CR), CR)

        @pl.when(z > 0)
        def _():
            chunk_copy(c).wait_recv()
            pm[rows, :] = pm[rows, :] + pr[rows, :]

        @pl.when(z < nr - 1)
        def _():
            chunk_copy(c).start()

        val = pm[rows, :]
        hi, lo = split(val)
        ph[rows, :] = hi
        plo[rows, :] = lo
        hi, lo = split(val * bar[...])
        sc[b, pl.ds(pl.multiple_of(i * CR, CR), CR), :] = hi
        sc[b, pl.ds(pl.multiple_of(BLK + i * CR, CR), CR), :] = lo

    def n_copy(b, src, dst):
        return pltpu.make_async_remote_copy(
            src_ref=nsend.at[b, dst], dst_ref=nrecv.at[b, src],
            send_sem=n_ssem.at[b, dst], recv_sem=n_rsem.at[b, src],
            device_id={"vars": dst}, device_id_type=MESH,
        )

    def d_copy(b, src, dst):
        width = BLK * (b + 1)
        return pltpu.make_async_remote_copy(
            src_ref=dsend.at[b, dst, :, pl.ds(0, width)],
            dst_ref=drecv.at[b, src, :, pl.ds(0, width)],
            send_sem=d_ssem.at[b, dst], recv_sem=d_rsem.at[b, src],
            device_id={"vars": dst}, device_id_type=MESH,
        )

    def g_copy(b, src, dst):
        width = BLK * (b + 1)
        ref = dsum.at[b, src, :, pl.ds(0, width)]
        return pltpu.make_async_remote_copy(
            src_ref=ref, dst_ref=ref,
            send_sem=g_ssem.at[b, dst], recv_sem=g_rsem.at[b, src],
            device_id={"vars": dst}, device_id_type=MESH,
        )

    def others(fn, count=None):
        @pl.loop(1, nv)
        def _(i):
            fn(lax.rem(v + i, nv))

    def diag_part(b):
        width = BLK * (b + 1)
        d = dot(sc[b], ph[pl.ds(0, width), :])
        d = d[:BLK] + (d[BLK:] + dot(sc[b, pl.ds(0, BLK), :], plo[pl.ds(0, width), :]))
        dsend[b, :, :, pl.ds(0, width)] = d.reshape(nred, dr, width)

        def send(dst):
            @pl.when(dst < nred)
            def _():
                d_copy(b, v, dst).start()

        others(send)

    def diag_reduce(b):
        width = BLK * (b + 1)

        @pl.when(v < nred)
        def _():
            dsum[b, v, :, pl.ds(0, width)] = dsend[b, v, :, pl.ds(0, width)]

            def add(src):
                d_copy(b, src, v).wait_recv()
                dsum[b, v, :, pl.ds(0, width)] += drecv[b, src, :, pl.ds(0, width)]

            others(add)
            others(lambda dst: g_copy(b, v, dst).start())

    def diag_finish(b):
        def get(src):
            @pl.when(src < nred)
            def _():
                g_copy(b, src, v).wait_recv()

        others(get)

        def diag(j):
            return dsum[b, :, :, pl.ds(j * BLK, BLK)].reshape(BLK, BLK)

        factor_start(b, diag, lower, inv, ws, wm)

    def product(b, part):
        arows = pl.ds(part * half, half)
        n = dot(ah[arows, :], sc[b])
        n = n[:, :BLK] + (n[:, BLK:] + dot(al[arows, :], sc[b, pl.ds(0, BLK), :]))
        per = nv // 2
        nsend[b, pl.ds(part * per, per)] = n.reshape(per, share, BLK)

        @pl.loop(part * per, (part + 1) * per)
        def _(dst):
            @pl.when(dst != v)
            def _():
                n_copy(b, v, dst).start()

    def solve(b):
        def add(src):
            n_copy(b, src, v).wait_recv()
            nsend[b, v] += nrecv[b, src]

        others(add)
        x = nsend[b, v]
        if b > 0:
            left = pl.ds(0, b * BLK)
            x -= dot6(x_out[:, left], lower[pl.ds(b * BLK, BLK), left], ((1,), (1,)))
        x_out[:, pl.ds(b * BLK, BLK)] = dot6(x, inv[b], ((1,), (1,)))

    def steps(b, low, high, also=None):
        @pl.loop(low, high)
        def _(i):
            if b < nblk:
                forward(b, i)
            if also is not None:
                also(i)

    def halves(i):
        for k in range(2):
            at = pl.multiple_of(((i - mid) * 2 + k) * per_step, per_step)
            rows = pl.ds(at, per_step)
            hi, lo = split(apad[rows, :])
            ah[rows, :] = hi
            al[rows, :] = lo

    per_step = rows_here // cpb
    mid = cpb // 2
    groups = BLK // GRP // (cpb - mid)
    own_copy(0).wait()
    steps(0, 0, mid)
    load.wait()
    steps(0, mid, cpb, halves)
    for b in range(1, nblk + 1):
        if b < nblk:
            own_copy(b).wait()
        diag_part(b - 1)
        steps(b, 0, 2)
        product(b - 1, 0)
        steps(b, 2, 3)
        diag_reduce(b - 1)
        steps(b, 3, mid)
        product(b - 1, 1)
        diag_finish(b - 1)

        def columns(i):
            for g in range(groups):
                eliminate(((i - mid) * groups + g) * GRP, ws, wm)

        steps(b, mid, cpb, columns)
        factor_end(b - 1, lower, inv, ws, wm)
        solve(b - 1)

    @pl.when(z < nr - 1)
    def _():
        @pl.loop(0, PANEL // CR)
        def _(c):
            chunk_copy(c).wait_send()

    for b in range(nblk):
        def drain(dst):
            n_copy(b, v, dst).wait_send()

            @pl.when(dst < nred)
            def _():
                d_copy(b, v, dst).wait_send()

            @pl.when(v < nred)
            def _():
                g_copy(b, v, dst).wait_send()

        others(drain)


def finish_kernel(share, pos, x_ref, l_hbm, o_ref, wide, sem):
    count = share + 8
    low = jnp.clip(pos[0], 0, PANEL - count)
    base = pl.multiple_of(low // 8 * 8, 8)
    copy = pltpu.make_async_copy(l_hbm.at[pl.ds(base, count)], wide, sem)
    copy.start()
    copy.wait()
    turn = lax.rem(lax.rem(base - pos[0], count) + count, count)
    row = pos[0] + lax.broadcasted_iota(jnp.int32, (share, 128), 0)
    inside = (row >= 0) & (row < PANEL)
    for j in range(0, PANEL, 128):
        part = pltpu.roll(wide[:, j:j + 128], turn, 0)[0:share]
        x = jnp.where(row >= PANEL, x_ref[:, j:j + 128], 0.0)
        o_ref[:, j:j + 128] = jnp.where(inside, part, x)


def body(nr, nv, matrix, barrier, panel_index, row_offset):
    rows_here, vloc = matrix.shape
    share = rows_here // nv
    nblk = PANEL // BLK
    nred = min(nv, BLK // 8)
    dr = BLK // nred
    first = panel_index * PANEL + row_offset
    vm = pl.BlockSpec(memory_space=pltpu.VMEM)
    sm = pl.BlockSpec(memory_space=pltpu.SMEM)
    dma = pltpu.SemaphoreType.DMA
    nchunk = PANEL // CR
    picked = pl.pallas_call(
        pick_kernel,
        out_shape=jax.ShapeDtypeStruct((PANEL, vloc), F32),
        in_specs=[sm, pl.BlockSpec(memory_space=pl.ANY)],
        out_specs=vm,
        scratch_shapes=[
            pltpu.VMEM((nblk, BLK + 8, vloc), F32),
            dma((nblk,)),
        ],
        compiler_params=pltpu.CompilerParams(vmem_limit_bytes=58 << 20),
        name="pick",
    )(first - lax.axis_index("rows") * rows_here, matrix)
    x, low = pl.pallas_call(
        functools.partial(panel_kernel, nr, nv, nred),
        out_shape=(
            jax.ShapeDtypeStruct((share, PANEL), F32),
            jax.ShapeDtypeStruct((PANEL, PANEL), F32),
        ),
        in_specs=[pl.BlockSpec(memory_space=pl.ANY), pl.BlockSpec(memory_space=pl.ANY), vm],
        out_specs=(vm, vm),
        scratch_shapes=[
            pltpu.VMEM((rows_here, vloc), F32),
            pltpu.VMEM((rows_here, vloc), BF16),
            pltpu.VMEM((rows_here, vloc), BF16),
            pltpu.VMEM((PANEL, vloc), F32),
            pltpu.VMEM((PANEL, vloc), F32),
            pltpu.VMEM((PANEL, vloc), BF16),
            pltpu.VMEM((PANEL, vloc), BF16),
            pltpu.VMEM((nblk, 2 * BLK, vloc), BF16),
            pltpu.VMEM((nblk, nv, share, BLK), F32),
            pltpu.VMEM((nblk, nv, share, BLK), F32),
            pltpu.VMEM((nblk, nred, dr, PANEL), F32),
            pltpu.VMEM((nblk, nv, dr, PANEL), F32),
            pltpu.VMEM((nblk, nred, dr, PANEL), F32),
            pltpu.VMEM((BLK, BLK), F32),
            pltpu.VMEM((BLK, BLK), F32),
            pltpu.VMEM((nblk, BLK, BLK), F32),
            dma,
            dma((nblk,)),
            dma((nchunk,)),
            dma((nchunk,)),
            dma((nblk, nv)),
            dma((nblk, nv)),
            dma((nblk, nv)),
            dma((nblk, nv)),
            dma((nblk, nv)),
            dma((nblk, nv)),
        ],
        compiler_params=pltpu.CompilerParams(
            collective_id=0, has_side_effects=True, vmem_limit_bytes=60 << 20
        ),
        name="panel_sums",
    )(picked, matrix, barrier.reshape(1, vloc))
    own = lax.axis_index("rows") * rows_here + lax.axis_index("vars") * share
    return pl.pallas_call(
        functools.partial(finish_kernel, share),
        out_shape=jax.ShapeDtypeStruct((share, PANEL), F32),
        in_specs=[sm, vm, pl.BlockSpec(memory_space=pl.ANY)],
        out_specs=vm,
        scratch_shapes=[pltpu.VMEM((share + 8, PANEL), F32), dma],
        name="finish",
    )(own - first, x, low)


def solution(mesh):
    return jax.shard_map(
        functools.partial(body, mesh.shape["rows"], mesh.shape["vars"]),
        mesh=mesh,
        in_specs=(P("rows", "vars"), P("vars"), P(), P()),
        out_specs=P(("rows", "vars"), None),
        check_vma=False,
    )
```
